256 devices in a mesh: lat: 4 (over x), lon: 2 (over core), ens: 32 (over z, y).
Axes of the slice: x: 4, y: 4, z: 8, core: 2. Of those that a mesh axis runs over, the one named last changes fastest.
Arguments:
- inputs: bfloat16 [32, 8, 1440, 256], P('ens', 'lat', 'lon'), may hold values from -12 to 12
- weight: bfloat16 [9, 256, 256], replicated, may hold values from -0.125 to 0.125
- spread: int32 [8], P('lat'), may hold values from 2 to 16, as said below
- target: bfloat16 [8, 1440, 256], P('lat', 'lon'), may hold values from -6 to 6
Outputs:
- response: bfloat16 [32, 8, 1440, 256], P('ens', 'lat', 'lon')
- grad_input: bfloat16 [32, 8, 1440, 256], P('ens', 'lat', 'lon')
- grad_weight: float32 [9, 256, 256], replicated
- loss: float32 [], replicated
The draws below stay inside these ranges and needn't reach their ends.
Inputs may be any that keep to these rules, and one draw needn't show every extreme that they name: The filter of row o spans 2 spread[o] + 1 longitudes; spread is 16 on the 2 polar rows at each pole, which ignore it, and on the next row toward the equator.
All inputs are finite; a program needn't handle non-finite values.
Results may differ from the reference program's by a relative error of at most 0.009.
Values may be sent and summed in bfloat16 or wider, within the bound.
No kernel may reach another device: no remote copies, remote signals or barrier semaphores. Data moves between devices by JAX's collectives and lax.ppermute only.
A program may use at most 128 MiB of HBM per device.

```python
import math
import jax
import jax.numpy as jnp
from jax import lax

C = 256
K = 9
PCAP = 2
HMAX = 16
LON_DEV = 720
E = 32
NLAT = 8
NLON = 1440


def draw_inputs(key, part):
    keys = jax.random.split(key, 4)
    shape = (E, NLAT, NLON, C)
    rough = jax.random.normal(keys[0], shape, jnp.float32)
    level = jax.random.normal(keys[1], (E, NLAT, 1, C), jnp.float32)
    amplitude = jax.random.normal(keys[2], (E, NLAT, 1, C), jnp.float32)
    phase = jax.random.uniform(keys[3], (E, NLAT, 1, C), jnp.float32, 0.0, 2.0 * math.pi)
    angles = 2.0 * math.pi * jnp.arange(NLON).astype(jnp.float32) / NLON
    lat_rows = jnp.arange(NLAT).astype(jnp.int32)
    distance = jnp.minimum(lat_rows, NLAT - 1 - lat_rows)
    cap_rows = (distance < PCAP - 1).astype(jnp.float32)[None, :, None, None]
    smooth = level + amplitude * jnp.cos(angles[None, None, :, None] - phase)
    field = rough + cap_rows * smooth
    return jnp.clip(field, -12.0, 12.0).astype(jnp.bfloat16)


def draw_spread(key, part):
    lat_rows = jnp.arange(NLAT).astype(jnp.int32)
    distance = jnp.minimum(lat_rows, NLAT - 1 - lat_rows)
    halfway = NLAT // 2
    baseline = 2 + (HMAX - 2) * (halfway - 1 - distance) // max(halfway - 1, 1)
    jitter = jax.random.randint(key, (NLAT,), 0, HMAX // 2 + 1)
    values = jnp.clip(baseline + jitter, 2, HMAX)
    values = jnp.where(lat_rows == halfway - 1, 2, values)
    values = jnp.where(distance <= PCAP, HMAX, values)
    return values.astype(jnp.int32)


def shard_levels(key, dims, cuts, smallest, largest):
    factor_of, own = 1.0, jax.random.fold_in(key, 6)
    for axis_at, parts in cuts:
        heights = jnp.exp(jax.random.uniform(jax.random.fold_in(own, axis_at), (parts,), jnp.float32, smallest / len(cuts), largest / len(cuts)))
        factor_of = factor_of * jnp.repeat(heights, dims[axis_at] // parts).reshape([-1 if axis == axis_at else 1 for axis in range(len(dims))])
    return factor_of


def scatter_about(rng, dims, scale, bound, cuts=(), kind=jnp.bfloat16):
    factor_of = shard_levels(rng, dims, cuts, -0.22, 0.18) if cuts else 1.0
    drawn = jax.random.normal(rng, dims, jnp.float32) * scale * factor_of
    return jnp.minimum(jnp.maximum(drawn, -bound), bound).astype(kind)


def setup_inputs(seed: int = 0) -> dict:
    seeds = jax.random.split(jax.random.key(seed), 5)
    inputs = draw_inputs(jax.random.fold_in(seeds[4], 71), 0)
    weight = scatter_about(seeds[1], (K, C, C), (K * C) ** -0.5, 0.125)
    spread = draw_spread(jax.random.fold_in(seeds[4], 71), 0)
    target = scatter_about(seeds[3], (NLAT, NLON, C), 1.0, 6.0, ((0, 4), (1, 2)))
    return dict(inputs=inputs, weight=weight, spread=spread, target=target)


highest = lax.Precision.HIGHEST

def kernel_rows(spread_rows, lon_count, reach):
    halves = spread_rows.astype(jnp.float32)[:, None, None, None] / 2.0
    columns = jnp.arange(lon_count)
    window_cols = jnp.arange(lon_count + 2 * reach)
    offsets = (window_cols[None, :] - reach - columns[:, None]).astype(jnp.float32)
    centres = (jnp.arange(3) - 1).astype(jnp.float32)[None, :, None, None] * halves
    values = jnp.maximum(0.0, 1.0 - jnp.abs(offsets[None, None] - centres) / halves) / halves
    return values.astype(jnp.bfloat16)

def circle_basis(first_col, lon_count, circle):
    angles = 2.0 * math.pi * (first_col + jnp.arange(lon_count)).astype(jnp.float32) / circle
    return jnp.stack([jnp.ones_like(angles), jnp.cos(angles), jnp.sin(angles)])

def circular(circle_sums, basis, circle, row_count):
    cos_wave = basis[1][None, None, :, None]
    sin_wave = basis[2][None, None, :, None]
    pieces = []
    for lat_tap in range(3):
        tap_sums = circle_sums[:, :, lat_tap:lat_tap + row_count]
        mean_part = tap_sums[:, 0][:, :, None, :] / circle
        cosine_part = 2.0 / circle * (cos_wave * tap_sums[:, 1][:, :, None, :] + sin_wave * tap_sums[:, 2][:, :, None, :])
        sine_part = 2.0 / circle * (cos_wave * tap_sums[:, 2][:, :, None, :] - sin_wave * tap_sums[:, 1][:, :, None, :])
        pieces += [jnp.broadcast_to(mean_part, cosine_part.shape), cosine_part, sine_part]
    return jnp.stack(pieces, 2)

def reference(inputs, weight, spread, target):
    members = inputs.shape[0]
    reach = HMAX
    padded = jnp.pad(inputs, ((0, 0), (1, 1), (0, 0), (0, 0)))
    padded = jnp.concatenate([padded[:, :, NLON - reach:], padded, padded[:, :, :reach]], 2)
    kernels = kernel_rows(spread, LON_DEV, reach).astype(jnp.float32)
    basis = circle_basis(0, NLON, NLON)
    lat_rows = jnp.arange(NLAT).astype(jnp.int32)
    polar_flags = (lat_rows < PCAP) | (lat_rows >= NLAT - PCAP)
    weight_wide = weight.astype(jnp.float32)

    def convolve(window_rows, kernel, flag):
        blocks = jnp.stack([window_rows[:, :, block_start:block_start + LON_DEV + 2 * reach] for block_start in range(0, NLON, LON_DEV)])
        banded = jnp.einsum('bjq,nerqc->erbnjc', kernel, blocks)
        banded = banded.reshape(members, K, NLON, C)
        centre = window_rows[:, :, reach:reach + NLON]
        circle_sums = jnp.einsum('pj,erjc->eprc', basis, centre, precision=highest)
        rounds = circular(circle_sums, basis, NLON, 1)[:, 0]
        return jnp.where(flag, rounds, banded)

    def forward_row(items):
        row_index, kernel, flag = items
        window_rows = lax.dynamic_slice_in_dim(padded, row_index, 3, 1).astype(jnp.float32)
        features = convolve(window_rows, kernel, flag).astype(jnp.bfloat16)
        return jnp.einsum('ekjc,kcd->ejd', features.astype(jnp.float32), weight_wide).astype(jnp.bfloat16)
    response = lax.map(forward_row, (lat_rows, kernels, polar_flags)).transpose(1, 0, 2, 3)
    values = response.astype(jnp.float32)
    truth = target.astype(jnp.float32)[None]
    miss = values - truth
    own_dist = jnp.sqrt(miss * miss + 0.25)
    own_slope = miss / own_dist
    pair_dist = jnp.zeros_like(values)
    pair_slope = jnp.zeros_like(values)
    for member in range(members):
        gap_value = values - values[member][None]
        distance = jnp.sqrt(gap_value * gap_value + 0.25)
        pair_dist = pair_dist + distance
        pair_slope = pair_slope + gap_value / distance
    pair_dist = pair_dist - 0.5
    lat_weight = jnp.sin(math.pi * (lat_rows.astype(jnp.float32) + 0.5) / NLAT)[None, :, None, None]
    scores = own_dist / members - pair_dist / (2 * members * (members - 1))
    loss = jnp.sum(lat_weight * scores) / (NLAT * NLON * C)
    slopes = (lat_weight * (own_slope / members - pair_slope / (members * (members - 1)))).astype(jnp.bfloat16)

    def backward_row(carry, items):
        grad_w, grad_x = carry
        row_index, kernel, flag, row_slopes = items
        window_rows = lax.dynamic_slice_in_dim(padded, row_index, 3, 1).astype(jnp.float32)
        features, pull_back = jax.vjp(lambda rows_in: convolve(rows_in, kernel, flag), window_rows)
        features = lax.optimization_barrier(features.astype(jnp.bfloat16)).astype(jnp.float32)
        slopes_wide = row_slopes.astype(jnp.float32)
        grad_w = grad_w + jnp.einsum('ekjc,ejd->kcd', features, slopes_wide)
        feature_grad = jnp.einsum('ejd,kcd->ekjc', slopes_wide, weight_wide)
        feature_grad = lax.optimization_barrier(feature_grad.astype(jnp.bfloat16)).astype(jnp.float32)
        row_grad, = pull_back(feature_grad)
        current = lax.dynamic_slice_in_dim(grad_x, row_index, 3, 1)
        grad_x = lax.dynamic_update_slice_in_dim(grad_x, current + row_grad, row_index, 1)
        return ((grad_w, grad_x), None)
    start_carry = (jnp.zeros((K, C, C), jnp.float32), jnp.zeros(padded.shape, jnp.float32))
    (grad_w, grad_x), _ = lax.scan(backward_row, start_carry, (lat_rows, kernels, polar_flags, slopes.transpose(1, 0, 2, 3)))
    core = grad_x[:, 1:NLAT + 1]
    inner = core[:, :, reach:reach + NLON]
    inner = inner.at[:, :, NLON - reach:].add(core[:, :, :reach])
    inner = inner.at[:, :, :reach].add(core[:, :, reach + NLON:])
    grad_weight = grad_w * math.sqrt(K * C) / (NLAT * NLON)
    return (response, inner.astype(jnp.bfloat16), grad_weight, loss)
```

```python
import functools
import math

import jax
import jax.numpy as jnp
import numpy as np
from jax import lax
from jax.experimental import pallas as pl
from jax.experimental.pallas import tpu as pltpu
from jax.sharding import PartitionSpec as P

PCAP = 2
HMAX = 16
BLK = 224
VMEM_LIMIT = 24 << 20
F32 = jnp.float32
BF16 = jnp.bfloat16


def split(values):
    high = lax.reduce_precision(values, 8, 7)
    return high.astype(BF16), (values - high).astype(BF16)


def dot(a, b, ca, cb):
    return lax.dot_general(a, b, (((ca,), (cb,)), ((), ())), preferred_element_type=F32)


def circle_waves(lon_index, lon_count, lon_total):
    angles = 2.0 * np.pi * np.arange(lon_total) / lon_total
    both = np.stack([np.cos(angles), np.sin(angles)])
    high = both.astype(BF16)
    low = (both - high.astype(np.float64)).astype(BF16)
    basis = np.concatenate([high, np.ones_like(high[:1]), low])
    columns = both.T.astype(np.float32).reshape(-1, lon_count, 2)
    basis = basis.reshape(5, -1, lon_count).transpose(1, 0, 2)
    pick = functools.partial(lax.dynamic_index_in_dim, index=lon_index, axis=0, keepdims=False)
    return pick(jnp.asarray(columns)), pick(jnp.asarray(basis))


def blocks(width):
    return [(start, min(BLK, width - start)) for start in range(0, width, BLK)]


def band_blocks(spread_rows, band_flags, reach):
    wide = spread_rows.astype(F32)[:, None, None, None]
    halves = jnp.where(wide > 0, wide, 2.0) / 2.0
    offsets = (jnp.arange(BLK + 2 * reach)[None, :] - reach - jnp.arange(BLK)[:, None]).astype(F32)
    centres = (jnp.arange(3) - 1).astype(F32)[None, :, None, None] * halves
    values = jnp.maximum(0.0, 1.0 - jnp.abs(offsets[None, None] - centres) / halves) / halves
    values = jnp.where(band_flags[:, None, None, None], values, 0.0)
    return values.astype(BF16)


def circle_parcel(rows, basis, reach):
    count, width, channels = rows.shape
    sums = jnp.einsum("pj,rjc->rpc", basis, rows, preferred_element_type=F32)
    sums = jnp.concatenate([sums[:, :2] + sums[:, 3:], sums[:, 2:3]], 1)
    high, low = split(sums)
    spare = jnp.zeros((count, reach - 6, channels), BF16)
    parcel = jnp.concatenate([rows[:, :reach], rows[:, width - reach :], high, low, spare], 1)
    return sums, lax.ppermute(parcel, "lon", [(0, 1), (1, 0)])


def extend_lon(rows, basis, spread_rows, reach):
    count, _, channels = rows.shape
    sums, other = circle_parcel(rows, basis, reach)
    total = sums + other[:, 2 * reach : 2 * reach + 3].astype(F32)
    total = total + other[:, 2 * reach + 3 : 2 * reach + 6].astype(F32)
    high, low = split(total)
    mark = jnp.broadcast_to(spread_rows.astype(BF16)[:, None, None], (count, reach - 6, channels))
    return jnp.concatenate(
        [other[:, reach : 2 * reach], rows, other[:, :reach], high, low, mark], 1
    )


def lat_neighbours(rows):
    count = lax.axis_size("lat")
    low = lax.ppermute(rows[-1:], "lat", [(i, i + 1) for i in range(count - 1)])
    high = lax.ppermute(rows[:1], "lat", [(i + 1, i) for i in range(count - 1)])
    return low, high


def convolved(row, pairs, weight_ref, band_ref, wave_ref, flag_ref):
    width = wave_ref.shape[0]
    circle = 2 * width
    reach = HMAX
    ext = width + 2 * reach
    extras = []
    total = [None] * len(blocks(width))
    for shape in range(3):
        mixed = None
        for source, tap in pairs:
            part = dot(source[...], weight_ref[3 * tap + shape], 1, 0)
            mixed = part if mixed is None else mixed + part
        extras.append(mixed[ext : ext + 3] + mixed[ext + 3 : ext + 6])
        mixed = mixed.astype(BF16)
        for part, (start, size) in enumerate(blocks(width)):
            piece = dot(
                band_ref[row, shape, :size, : size + 2 * reach],
                mixed[start : start + size + 2 * reach],
                1,
                0,
            )
            total[part] = piece if shape == 0 else total[part] + piece
    polar = flag_ref[row]
    flat = extras[0][2:3] * (polar / circle)
    with_cos = (extras[1][0:1] + extras[2][1:2]) * (polar * 2.0 / circle)
    with_sin = (extras[1][1:2] - extras[2][0:1]) * (polar * 2.0 / circle)
    answers = []
    for part, (start, size) in enumerate(blocks(width)):
        at = pl.ds(start, size)
        answers.append(
            total[part] + (flat + wave_ref[at, 0:1] * with_cos + wave_ref[at, 1:2] * with_sin)
        )
    return answers


def own_rows_kernel(own_ref, weight_ref, band_ref, wave_ref, flag_ref, out_ref):
    for row in range(2):
        pairs = [(own_ref.at[0], 1 - row), (own_ref.at[1], 2 - row)]
        parts = convolved(row, pairs, weight_ref, band_ref, wave_ref, flag_ref)
        for (start, size), part in zip(blocks(wave_ref.shape[0]), parts):
            out_ref[row, pl.ds(start, size)] = part


def outer_rows_kernel(
    low_ref, high_ref, begun_ref, weight_ref, band_ref, wave_ref, flag_ref, out_ref, sent_ref
):
    width = wave_ref.shape[0]
    for row, source, tap in ((0, low_ref, 0), (1, high_ref, 2)):
        parts = convolved(row, [(source.at[0], tap)], weight_ref, band_ref, wave_ref, flag_ref)
        for (start, size), part in zip(blocks(width), parts):
            answer = (begun_ref[row, pl.ds(start, size)] + part).astype(BF16)
            out_ref[row, pl.ds(start, size)] = answer
            sent_ref[pl.ds(row * width + start, size)] = answer
    spare = sent_ref.shape[0] - 2 * width
    sent_ref[2 * width :] = jnp.zeros((spare, sent_ref.shape[1]), BF16)


def spread_back_rows(ext_row, row, band_ref, wave_ref, polar):
    width = wave_ref.shape[0]
    circle = 2 * width
    reach = HMAX
    ext = width + 2 * reach
    sums = ext_row[ext : ext + 16, :].astype(F32)
    sums = (sums[0:3] + sums[3:6]) * polar
    cos_sum, sin_sum, flat = sums[0:1] * (2.0 / circle), sums[1:2] * (2.0 / circle), sums[2:3]
    flat = flat / circle
    answers = []
    for shape in range(3):
        pieces = []
        for start, size in blocks(width):
            piece = dot(
                band_ref[row, 2 - shape, :size, : size + 2 * reach],
                ext_row[pl.ds(start, size + 2 * reach), :],
                1,
                0,
            )
            at = pl.ds(start, size)
            cos_wave, sin_wave = wave_ref[at, 0:1], wave_ref[at, 1:2]
            if shape == 0:
                piece = piece + flat
            elif shape == 1:
                piece = piece + (cos_wave * cos_sum + sin_wave * sin_sum)
            else:
                piece = piece + (sin_wave * cos_sum - cos_wave * sin_sum)
            pieces.append(piece.astype(BF16))
        answers.append(jnp.concatenate(pieces, 0))
    return answers


def weight_grad_kernel(
    slope_ref,
    sums_ref,
    other_ref,
    low_ref,
    own_ref,
    high_ref,
    band_ref,
    wave_ref,
    flag_ref,
    lon_ref,
    spread_ref,
    mine_ref,
    theirs_ref,
    ext_ref,
    back_ref,
    field_ref,
    sems,
    *,
    scale,
):
    width = wave_ref.shape[0]
    reach = HMAX
    inner = pl.ds(reach, width)
    channels = low_ref.shape[-1]
    copies = [
        pltpu.make_async_copy(slope_ref.at[pl.ds(0, width)], ext_ref.at[0, inner], sems.at[0]),
        pltpu.make_async_copy(slope_ref.at[pl.ds(width, width)], ext_ref.at[1, inner], sems.at[1]),
        pltpu.make_async_copy(low_ref.at[0, inner], field_ref.at[0], sems.at[2]),
        pltpu.make_async_copy(own_ref.at[0, inner], field_ref.at[1], sems.at[3]),
        pltpu.make_async_copy(own_ref.at[1, inner], field_ref.at[2], sems.at[4]),
        pltpu.make_async_copy(high_ref.at[0, inner], field_ref.at[3], sems.at[5]),
    ]
    for copy in copies:
        copy.start()
    for row in range(2):
        total = sums_ref[row] + other_ref[row, 2 * reach : 2 * reach + 3].astype(F32)
        total = total + other_ref[row, 2 * reach + 3 : 2 * reach + 6].astype(F32)
        high = total.astype(BF16)
        low = (total - high.astype(F32)).astype(BF16)
        mark = jnp.full((reach - 6, channels), spread_ref[row], F32).astype(BF16)
        ext_ref[row, :reach] = other_ref[row, reach : 2 * reach]
        ext_ref[row, reach + width : 2 * reach + width] = other_ref[row, :reach]
        ext_ref[row, 2 * reach + width :] = jnp.concatenate([high, low, mark], 0)
    for row in range(2):
        copies[row].wait()
        backs = spread_back_rows(ext_ref.at[row], row, band_ref, wave_ref, flag_ref[row])
        for shape in range(3):
            back_ref[row, :, shape * channels : (shape + 1) * channels] = backs[shape]
    for copy in copies[2:]:
        copy.wait()
    half = mine_ref.shape[0] // 2
    lanes = channels // 2
    for tap in range(3):
        part = dot(field_ref[tap], back_ref[0], 0, 0)
        part = ((part + dot(field_ref[tap + 1], back_ref[1], 0, 0)) * scale).astype(BF16)
        for shape in range(3):
            first = (3 * tap + shape) * channels
            for start in range(0, channels, channels // 2):
                owner, at = divmod(first + start, half)
                for side in range(2):
                    left = shape * channels + side * lanes
                    piece = part[start : start + channels // 2, left : left + lanes]
                    into = pl.ds(side * half + at, channels // 2)

                    @pl.when(lon_ref[0] == owner)
                    def _():
                        mine_ref[into] = piece

                    @pl.when(lon_ref[0] != owner)
                    def _():
                        theirs_ref[into] = piece


def merge_kernel(mine_ref, theirs_ref, loss_ref, out_ref):
    count, rows, _ = out_ref.shape
    piece = mine_ref.shape[0] // count
    share = loss_ref[...]
    high = share.astype(BF16)
    low = (share - high.astype(F32)).astype(BF16)
    blank = jnp.zeros((rows - piece - 2, out_ref.shape[2]), BF16)
    mark = jnp.concatenate([high, low, blank], 0)
    for i in range(count):
        at = pl.ds(i * piece, piece)
        total = mine_ref[at].astype(F32) + theirs_ref[at].astype(F32)
        out_ref[i, :piece] = total.astype(BF16)
        out_ref[i, piece:] = mark


def whole_kernel(own_ref, other_ref, lon_ref, out_ref, loss_ref):
    count, _, lanes = own_ref.shape
    half = out_ref.shape[0] // 2
    side_count = count // 2
    piece = half // side_count
    for source, owner in ((own_ref, lon_ref[0]), (other_ref, 1 - lon_ref[0])):
        base = owner * half
        for i in range(count):
            side, at = divmod(i, side_count)
            into = pl.ds(pl.multiple_of(base + at * piece, 8), piece)
            out_ref[into, side * lanes : (side + 1) * lanes] = source[i, :piece].astype(F32)
    shares = own_ref[0, piece : piece + 2].astype(F32) + other_ref[0, piece : piece + 2].astype(F32)
    loss_ref[0, 0] = jnp.sum(shares)


def input_grad_kernel(
    low_ref, own_ref, high_ref, weight_ref, band_ref, wave_ref, flag_ref, out_ref, sum_ref
):
    rows = (low_ref.at[0], own_ref.at[0], own_ref.at[1], high_ref.at[0])
    for row in range(4):
        backs = spread_back_rows(rows[row], row, band_ref, wave_ref, flag_ref[row])
        for target in range(2):
            tap = target - row + 2
            if tap < 0 or tap > 2:
                continue
            part = dot(backs[0], weight_ref[3 * tap], 1, 1)
            for shape in (1, 2):
                part += dot(backs[shape], weight_ref[3 * tap + shape], 1, 1)
            if tap == 2:
                sum_ref[target] = part
            elif tap == 1:
                sum_ref[target] += part
            else:
                out_ref[target] = (sum_ref[target] + part).astype(BF16)


def crps_kernel(z_ref, truth_ref, weight_ref, slope_ref, loss_ref, value_ref, grad_ref):
    members, count, channels = z_ref.shape
    lat_weight = weight_ref[0]
    group = 8
    pair_scale = -1.0 / (members * (members - 1))
    value_ref[...] = z_ref[...].astype(F32)

    def tile(index, total):
        first = pl.multiple_of((index // (channels // 128)) * 8, 8)
        lane = pl.multiple_of((index % (channels // 128)) * 128, 128)
        at = (pl.ds(first, 8), pl.ds(lane, 128))
        truth = truth_ref[at].astype(F32)
        own = jnp.zeros((8, 128), F32)
        pair = jnp.zeros((8, 128), F32)
        moment = jnp.zeros((8, 128), F32)
        for start in range(0, members, group):
            values = [value_ref[(start + i, *at)] for i in range(group)]
            if start == 0:
                grads = [jnp.zeros((8, 128), F32) for _ in range(group)]
            else:
                grads = [grad_ref[(start + i, *at)] for i in range(group)]
            for i in range(group):
                for k in range(i):
                    gap = values[i] - values[k]
                    square = gap * gap + 0.25
                    inverse = lax.rsqrt(square)
                    pair = pair + inverse
                    slope = gap * inverse
                    grads[i] = grads[i] + slope
                    grads[k] = grads[k] - slope
            for m in range(start + group, members):
                other = value_ref[(m, *at)]
                if start == 0:
                    other_grad = jnp.zeros((8, 128), F32)
                else:
                    other_grad = grad_ref[(m, *at)]
                for i in range(group):
                    gap = other - values[i]
                    square = gap * gap + 0.25
                    inverse = lax.rsqrt(square)
                    pair = pair + inverse
                    slope = gap * inverse
                    other_grad = other_grad + slope
                    grads[i] = grads[i] - slope
                grad_ref[(m, *at)] = other_grad
            for i in range(group):
                miss = values[i] - truth
                square = miss * miss + 0.25
                inverse = lax.rsqrt(square)
                own = own + square * inverse
                moment = moment + values[i] * grads[i]
                answer = (miss * inverse) * (1.0 / members) + grads[i] * pair_scale
                grad_ref[(start + i, *at)] = answer * lat_weight
        pair = moment + 0.25 * pair
        return total + (own * (1.0 / members) + pair * pair_scale)

    tiles = (count // 8) * (channels // 128)
    total = lax.fori_loop(0, tiles, tile, jnp.zeros((8, 128), F32))
    loss_ref[...] = total * lat_weight
    slope_ref[...] = grad_ref[...].astype(BF16)


def call(kernel, out_shape, *operands, smem=(), smem_out=(), away=(), loose=False, scratch=(), held=()):
    spaces = [pltpu.VMEM for _ in operands]
    for i in smem:
        spaces[i] = pltpu.SMEM
    for i in away:
        spaces[i] = pl.ANY
    operands = [
        pltpu.with_memory_space_constraint(x, pltpu.VMEM)
        if space == pltpu.VMEM and not loose
        else x
        for x, space in zip(operands, spaces)
    ]
    shapes = [
        shape if loose else (pltpu.VMEM if i in held else pltpu.HBM)(shape.shape, shape.dtype)
        for i, shape in enumerate(out_shape)
    ]
    out_spaces = [pltpu.SMEM if i in smem_out else pltpu.VMEM for i in range(len(shapes))]
    return pl.pallas_call(
        kernel,
        out_shape=shapes,
        in_specs=[pl.BlockSpec(memory_space=space) for space in spaces],
        out_specs=[pl.BlockSpec(memory_space=space) for space in out_spaces],
        scratch_shapes=scratch,
        compiler_params=pltpu.CompilerParams(vmem_limit_bytes=None if loose else VMEM_LIMIT),
    )(*operands)


def reduce_weight_grad(mine, theirs, loss):
    lat_count, ens_count = lax.axis_size("lat"), lax.axis_size("ens")
    lon_index = lax.axis_index("lon")
    rows, lanes = mine.shape
    piece = rows // ens_count
    swap = [(0, 1), (1, 0)]
    arrived = lax.ppermute(theirs, "lon", swap)
    (summed,) = call(
        merge_kernel,
        (jax.ShapeDtypeStruct((ens_count, piece + 8, lanes), BF16),),
        mine,
        arrived,
        loss,
        loose=True,
    )
    summed = lax.all_to_all(summed, "ens", 0, 0, tiled=True)

    def marked(total):
        share = total[piece : piece + 1] + total[piece + 1 : piece + 2]
        blank = jnp.zeros((6, lanes), BF16)
        return jnp.concatenate([total[:piece].astype(BF16), *split(share), blank], 0)

    total = jnp.sum(summed.astype(F32), 0)
    sent = marked(total)
    arrived = [
        lax.ppermute(sent, "lat", [(i, (i + step) % lat_count) for i in range(lat_count)])
        for step in range(1, lat_count)
    ]
    for block in arrived:
        total = total + block.astype(F32)
    spread_out = jnp.broadcast_to(marked(total)[None], summed.shape)
    gathered = lax.all_to_all(spread_out, "ens", 0, 0, tiled=True)
    other = lax.ppermute(gathered, "lon", swap)
    whole, loss = call(
        whole_kernel,
        (
            jax.ShapeDtypeStruct((rows, 2 * lanes), F32),
            jax.ShapeDtypeStruct((1, 1), F32),
        ),
        gathered,
        other,
        lon_index[None],
        smem=(2,),
        smem_out=(1,),
        loose=True,
    )
    return whole, loss[0, 0]


def step(inputs, weight, spread, target):
    row_count, width, channels = inputs.shape[1:]
    reach = HMAX
    members = lax.axis_size("ens")
    lat_total = row_count * lax.axis_size("lat")
    lon_total = width * lax.axis_size("lon")
    lat_index, lon_index, ens_index = (lax.axis_index(a) for a in ("lat", "lon", "ens"))
    field = inputs[0]
    wave_cols, basis = circle_waves(lon_index, width, lon_total)
    rows_around = lat_index * row_count - 1 + jnp.arange(row_count + 2)
    polar = (rows_around < PCAP) | (rows_around >= lat_total - PCAP)
    polar_scale = polar.astype(F32)

    own = extend_lon(field, basis, spread, reach)
    low, high = lat_neighbours(own)
    own_band = band_blocks(spread, ~polar[1:3], reach)
    own_polar = polar_scale[1:3]
    cells = -(-(row_count * width // members) // 16) * 16
    (begun,) = call(
        own_rows_kernel,
        (jax.ShapeDtypeStruct((row_count, width, channels), F32),),
        own,
        weight,
        own_band,
        wave_cols,
        own_polar,
        smem=(4,),
        held=(0,),
    )
    response, sent = call(
        outer_rows_kernel,
        (
            jax.ShapeDtypeStruct((row_count, width, channels), BF16),
            jax.ShapeDtypeStruct((members * cells, channels), BF16),
        ),
        low,
        high,
        begun,
        weight,
        own_band,
        wave_cols,
        own_polar,
        smem=(6,),
    )
    everyone = lax.all_to_all(
        sent.reshape(members, cells, channels), "ens", 0, 0, tiled=True
    )
    held = row_count * width // cells
    first_cell = jnp.minimum(ens_index, held - 1) * cells
    truth = lax.dynamic_slice_in_dim(target.reshape(-1, channels), first_cell, cells, 0)
    cell_row = lat_index * row_count + first_cell // width
    row_weight = jnp.sin(math.pi * (cell_row.astype(F32) + 0.5) / lat_total)
    row_weight = jnp.where(ens_index < held, row_weight, 0.0)
    slopes, loss_tile = call(
        crps_kernel,
        (
            jax.ShapeDtypeStruct((members, cells, channels), BF16),
            jax.ShapeDtypeStruct((8, 128), F32),
        ),
        everyone,
        truth,
        row_weight[None],
        smem=(2,),
        held=(0, 1),
        scratch=[
            pltpu.VMEM((members, cells, channels), F32),
            pltpu.VMEM((members, cells, channels), F32),
        ],
    )
    slopes = lax.all_to_all(slopes, "ens", 0, 0, tiled=True)
    slopes = slopes.reshape(-1, channels)
    loss_share = jnp.sum(loss_tile, 0, keepdims=True) / (lat_total * lon_total * channels)

    slope_rows = slopes[: row_count * width].reshape(row_count, width, channels)
    slope_sums, slope_other = circle_parcel(slope_rows, basis, reach)
    scale = math.sqrt(weight.shape[0] * channels) / (lat_total * lon_total)
    half = jax.ShapeDtypeStruct((weight.shape[0] * channels, channels // 2), BF16)
    mine, theirs, slope_own = call(
        functools.partial(weight_grad_kernel, scale=scale),
        (half, half, jax.ShapeDtypeStruct((row_count, width + 3 * reach, channels), BF16)),
        slopes,
        slope_sums,
        slope_other,
        low,
        own,
        high,
        own_band,
        wave_cols,
        own_polar,
        lon_index[None],
        spread.astype(F32),
        smem=(8, 9, 10),
        away=(0, 3, 4, 5),
        loose=True,
        scratch=[
            pltpu.VMEM((row_count, width, 3 * channels), BF16),
            pltpu.VMEM((row_count + 2, width, channels), BF16),
            pltpu.SemaphoreType.DMA((6,)),
        ],
    )
    slope_low, slope_high = lat_neighbours(slope_own)
    grad_weight, loss = reduce_weight_grad(mine, theirs, loss_share)
    around = jnp.stack([low[0, -1, 0], high[0, -1, 0]]).astype(spread.dtype)
    all_spread = jnp.concatenate([around[:1], spread, around[1:]])
    (grad_input,) = call(
        input_grad_kernel,
        (jax.ShapeDtypeStruct((row_count, width, channels), BF16),),
        slope_low,
        slope_own,
        slope_high,
        weight,
        band_blocks(all_spread, ~polar, reach),
        wave_cols,
        polar_scale,
        smem=(6,),
        loose=True,
        scratch=[pltpu.VMEM((row_count, width, channels), F32)],
    )
    return (response[None], grad_input[None], grad_weight.reshape(weight.shape), loss)


def solution(mesh):
    in_specs = (P("ens", "lat", "lon", None), P(), P("lat"), P("lat", "lon", None))
    out_specs = (P("ens", "lat", "lon", None), P("ens", "lat", "lon", None), P(), P())
    return jax.shard_map(step, mesh=mesh, in_specs=in_specs, out_specs=out_specs, check_vma=False)
```

```python
import functools
import math

import jax
import jax.numpy as jnp
import numpy as np
from jax import lax
from jax.experimental import pallas as pl
from jax.experimental.pallas import tpu as pltpu
from jax.sharding import PartitionSpec as P

PCAP = 2
HMAX = 16
BLK = 224
VMEM_LIMIT = 24 << 20
F32 = jnp.float32
BF16 = jnp.bfloat16


def split(values):
    high = lax.reduce_precision(values, 8, 7)
    return high.astype(BF16), (values - high).astype(BF16)


def dot(a, b, ca, cb):
    return lax.dot_general(a, b, (((ca,), (cb,)), ((), ())), preferred_element_type=F32)


def circle_waves(lon_index, lon_count, lon_total):
    angles = 2.0 * np.pi * np.arange(lon_total) / lon_total
    both = np.stack([np.cos(angles), np.sin(angles)])
    high = both.astype(BF16)
    low = (both - high.astype(np.float64)).astype(BF16)
    basis = np.concatenate([high, np.ones_like(high[:1]), low])
    columns = both.T.astype(np.float32).reshape(-1, lon_count, 2)
    basis = basis.reshape(5, -1, lon_count).transpose(1, 0, 2)
    pick = functools.partial(lax.dynamic_index_in_dim, index=lon_index, axis=0, keepdims=False)
    basis = jnp.asarray(basis)
    return pick(jnp.asarray(columns)), pick(basis), basis


def blocks(width):
    return [(start, min(BLK, width - start)) for start in range(0, width, BLK)]


def band_blocks(spread_rows, band_flags, reach):
    wide = spread_rows.astype(F32)[:, None, None, None]
    halves = jnp.where(wide > 0, wide, 2.0) / 2.0
    offsets = (jnp.arange(BLK + 2 * reach)[None, :] - reach - jnp.arange(BLK)[:, None]).astype(F32)
    centres = (jnp.arange(3) - 1).astype(F32)[None, :, None, None] * halves
    values = jnp.maximum(0.0, 1.0 - jnp.abs(offsets[None, None] - centres) / halves) / halves
    values = jnp.where(band_flags[:, None, None, None], values, 0.0)
    return values.astype(BF16)


def circle_parcel(rows, basis, reach):
    count, width, channels = rows.shape
    sums = jnp.einsum("pj,rjc->rpc", basis, rows, preferred_element_type=F32)
    sums = jnp.concatenate([sums[:, :2] + sums[:, 3:], sums[:, 2:3]], 1)
    high, low = split(sums)
    spare = jnp.zeros((count, reach - 6, channels), BF16)
    parcel = jnp.concatenate([rows[:, :reach], rows[:, width - reach :], high, low, spare], 1)
    return sums, lax.ppermute(parcel, "lon", [(0, 1), (1, 0)])


def parcel_kernel(field_ref, basis_ref, lon_ref, sums_ref, parcel_ref):
    width, channels = field_ref.shape[1:]
    reach = HMAX
    basis = basis_ref[lon_ref[0]]
    for row in range(2):
        parts = dot(basis, field_ref[row], 1, 0)
        sums = jnp.concatenate([parts[:2] + parts[3:5], parts[2:3]], 0)
        high = sums.astype(BF16)
        low = (sums - high.astype(F32)).astype(BF16)
        sums_ref[row] = sums
        parcel_ref[row, :reach] = field_ref[row, :reach]
        parcel_ref[row, reach : 2 * reach] = field_ref[row, width - reach :]
        parcel_ref[row, 2 * reach :] = jnp.concatenate(
            [high, low, jnp.zeros((reach - 6, channels), BF16)], 0
        )


def fill_edges(ext_ref, sums, other_ref, spread_row):
    reach = HMAX
    channels = ext_ref.shape[1]
    width = ext_ref.shape[0] - 3 * reach
    total = sums + other_ref[2 * reach : 2 * reach + 3].astype(F32)
    total = total + other_ref[2 * reach + 3 : 2 * reach + 6].astype(F32)
    high = total.astype(BF16)
    low = (total - high.astype(F32)).astype(BF16)
    mark = jnp.full((reach - 6, channels), spread_row, F32).astype(BF16)
    ext_ref[:reach] = other_ref[reach : 2 * reach]
    ext_ref[reach + width : 2 * reach + width] = other_ref[:reach]
    ext_ref[2 * reach + width :] = jnp.concatenate([high, low, mark], 0)


def extend_kernel(field_ref, sums_ref, other_ref, spread_ref, ext_ref):
    width = field_ref.shape[1]
    for row in range(2):
        fill_edges(ext_ref.at[row], sums_ref[row], other_ref.at[row], spread_ref[row])
        ext_ref[row, HMAX : HMAX + width] = field_ref[row]


def lat_neighbours(rows):
    count = lax.axis_size("lat")
    low = lax.ppermute(rows[-1:], "lat", [(i, i + 1) for i in range(count - 1)])
    high = lax.ppermute(rows[:1], "lat", [(i + 1, i) for i in range(count - 1)])
    return low, high


def convolved(row, pairs, weight_ref, band_ref, wave_ref, flag_ref):
    width = wave_ref.shape[0]
    circle = 2 * width
    reach = HMAX
    ext = width + 2 * reach
    extras = []
    total = [None] * len(blocks(width))
    for shape in range(3):
        mixed = None
        for source, tap in pairs:
            part = dot(source[...], weight_ref[3 * tap + shape], 1, 0)
            mixed = part if mixed is None else mixed + part
        extras.append(mixed[ext : ext + 3] + mixed[ext + 3 : ext + 6])
        mixed = mixed.astype(BF16)
        for part, (start, size) in enumerate(blocks(width)):
            piece = dot(
                band_ref[row, shape, :size, : size + 2 * reach],
                mixed[start : start + size + 2 * reach],
                1,
                0,
            )
            total[part] = piece if shape == 0 else total[part] + piece
    polar = flag_ref[row]
    flat = extras[0][2:3] * (polar / circle)
    with_cos = (extras[1][0:1] + extras[2][1:2]) * (polar * 2.0 / circle)
    with_sin = (extras[1][1:2] - extras[2][0:1]) * (polar * 2.0 / circle)
    answers = []
    for part, (start, size) in enumerate(blocks(width)):
        at = pl.ds(start, size)
        answers.append(
            total[part] + (flat + wave_ref[at, 0:1] * with_cos + wave_ref[at, 1:2] * with_sin)
        )
    return answers


def own_rows_kernel(own_ref, weight_ref, band_ref, wave_ref, flag_ref, out_ref):
    for row in range(2):
        pairs = [(own_ref.at[0], 1 - row), (own_ref.at[1], 2 - row)]
        parts = convolved(row, pairs, weight_ref, band_ref, wave_ref, flag_ref)
        for (start, size), part in zip(blocks(wave_ref.shape[0]), parts):
            out_ref[row, pl.ds(start, size)] = part


def outer_rows_kernel(
    low_ref, high_ref, begun_ref, weight_ref, band_ref, wave_ref, flag_ref, out_ref, sent_ref
):
    width = wave_ref.shape[0]
    for row, source, tap in ((0, low_ref, 0), (1, high_ref, 2)):
        parts = convolved(row, [(source.at[0], tap)], weight_ref, band_ref, wave_ref, flag_ref)
        for (start, size), part in zip(blocks(width), parts):
            answer = (begun_ref[row, pl.ds(start, size)] + part).astype(BF16)
            out_ref[row, pl.ds(start, size)] = answer
            sent_ref[pl.ds(row * width + start, size)] = answer
    spare = sent_ref.shape[0] - 2 * width
    sent_ref[2 * width :] = jnp.zeros((spare, sent_ref.shape[1]), BF16)


def spread_back_rows(ext_row, row, band_ref, wave_ref, polar):
    width = wave_ref.shape[0]
    circle = 2 * width
    reach = HMAX
    ext = width + 2 * reach
    sums = ext_row[ext : ext + 16, :].astype(F32)
    sums = (sums[0:3] + sums[3:6]) * polar
    cos_sum, sin_sum, flat = sums[0:1] * (2.0 / circle), sums[1:2] * (2.0 / circle), sums[2:3]
    flat = flat / circle
    answers = []
    for shape in range(3):
        pieces = []
        for start, size in blocks(width):
            piece = dot(
                band_ref[row, 2 - shape, :size, : size + 2 * reach],
                ext_row[pl.ds(start, size + 2 * reach), :],
                1,
                0,
            )
            at = pl.ds(start, size)
            cos_wave, sin_wave = wave_ref[at, 0:1], wave_ref[at, 1:2]
            if shape == 0:
                piece = piece + flat
            elif shape == 1:
                piece = piece + (cos_wave * cos_sum + sin_wave * sin_sum)
            else:
                piece = piece + (sin_wave * cos_sum - cos_wave * sin_sum)
            pieces.append(piece.astype(BF16))
        answers.append(jnp.concatenate(pieces, 0))
    return answers


def weight_grad_kernel(
    slope_ref,
    sums_ref,
    other_ref,
    low_ref,
    own_ref,
    high_ref,
    band_ref,
    wave_ref,
    flag_ref,
    lon_ref,
    spread_ref,
    mine_ref,
    theirs_ref,
    ext_ref,
    back_ref,
    field_ref,
    both_ref,
    sems,
    *,
    scale,
):
    width = wave_ref.shape[0]
    reach = HMAX
    inner = pl.ds(reach, width)
    channels = low_ref.shape[-1]
    copies = [
        pltpu.make_async_copy(slope_ref.at[pl.ds(0, width)], ext_ref.at[0, inner], sems.at[0]),
        pltpu.make_async_copy(slope_ref.at[pl.ds(width, width)], ext_ref.at[1, inner], sems.at[1]),
        pltpu.make_async_copy(low_ref.at[0, inner], field_ref.at[0], sems.at[2]),
        pltpu.make_async_copy(own_ref.at[0, inner], field_ref.at[1], sems.at[3]),
        pltpu.make_async_copy(own_ref.at[1, inner], field_ref.at[2], sems.at[4]),
        pltpu.make_async_copy(high_ref.at[0, inner], field_ref.at[3], sems.at[5]),
    ]
    for copy in copies:
        copy.start()
    for row in range(2):
        fill_edges(ext_ref.at[row], sums_ref[row], other_ref.at[row], spread_ref[row])
    for row in range(2):
        copies[row].wait()
        backs = spread_back_rows(ext_ref.at[row], row, band_ref, wave_ref, flag_ref[row])
        for shape in range(3):
            back_ref[row, :, shape * channels : (shape + 1) * channels] = backs[shape]
    for copy in copies[2:]:
        copy.wait()
    half = mine_ref.shape[0] // 2
    lanes = channels // 2
    for tap in range(3):
        part = dot(field_ref[tap], back_ref[0], 0, 0)
        part = ((part + dot(field_ref[tap + 1], back_ref[1], 0, 0)) * scale).astype(BF16)
        for shape in range(3):
            first = (3 * tap + shape) * channels
            for start in range(0, channels, channels // 2):
                owner, at = divmod(first + start, half)
                for side in range(2):
                    left = shape * channels + side * lanes
                    which = lon_ref[0] if owner == 0 else 1 - lon_ref[0]
                    into = (which, pl.ds(side * half + at, channels // 2))
                    both_ref[into] = part[start : start + channels // 2, left : left + lanes]
    leave = [
        pltpu.make_async_copy(both_ref.at[0], mine_ref, sems.at[6]),
        pltpu.make_async_copy(both_ref.at[1], theirs_ref, sems.at[7]),
    ]
    for copy in leave:
        copy.start()
    for copy in leave:
        copy.wait()


def merge_kernel(mine_ref, theirs_ref, loss_ref, out_ref):
    count, rows, _ = out_ref.shape
    piece = mine_ref.shape[0] // count
    share = loss_ref[...]
    high = share.astype(BF16)
    low = (share - high.astype(F32)).astype(BF16)
    blank = jnp.zeros((rows - piece - 2, out_ref.shape[2]), BF16)
    mark = jnp.concatenate([high, low, blank], 0)
    for i in range(count):
        at = pl.ds(i * piece, piece)
        total = mine_ref[at].astype(F32) + theirs_ref[at].astype(F32)
        out_ref[i, :piece] = total.astype(BF16)
        out_ref[i, piece:] = mark


def whole_kernel(own_ref, other_ref, lon_ref, out_ref):
    count, piece, lanes = own_ref.shape
    half = out_ref.shape[0] // 2
    side_count = count // 2
    for source, owner in ((own_ref, lon_ref[0]), (other_ref, 1 - lon_ref[0])):
        base = owner * half
        for i in range(count):
            side, at = divmod(i, side_count)
            into = pl.ds(pl.multiple_of(base + at * piece, 8), piece)
            out_ref[into, side * lanes : (side + 1) * lanes] = source[i].astype(F32)


def input_grad_kernel(
    low_ref, own_ref, high_ref, weight_ref, band_ref, wave_ref, flag_ref, out_ref, sum_ref
):
    rows = (low_ref.at[0], own_ref.at[0], own_ref.at[1], high_ref.at[0])
    for row in range(4):
        backs = spread_back_rows(rows[row], row, band_ref, wave_ref, flag_ref[row])
        for target in range(2):
            tap = target - row + 2
            if tap < 0 or tap > 2:
                continue
            part = dot(backs[0], weight_ref[3 * tap], 1, 1)
            for shape in (1, 2):
                part += dot(backs[shape], weight_ref[3 * tap + shape], 1, 1)
            if tap == 2:
                sum_ref[target] = part
            elif tap == 1:
                sum_ref[target] += part
            else:
                out_ref[target] = (sum_ref[target] + part).astype(BF16)


def crps_kernel(z_ref, truth_ref, weight_ref, slope_ref, loss_ref, value_ref, grad_ref):
    members, count, channels = z_ref.shape
    lat_weight = weight_ref[0]
    group = 8
    pair_scale = -1.0 / (members * (members - 1))
    value_ref[...] = z_ref[...].astype(F32)

    def tile(index, total):
        first = pl.multiple_of((index // (channels // 128)) * 8, 8)
        lane = pl.multiple_of((index % (channels // 128)) * 128, 128)
        at = (pl.ds(first, 8), pl.ds(lane, 128))
        truth = truth_ref[at].astype(F32)
        own = jnp.zeros((8, 128), F32)
        pair = jnp.zeros((8, 128), F32)
        moment = jnp.zeros((8, 128), F32)
        for start in range(0, members, group):
            values = [value_ref[(start + i, *at)] for i in range(group)]
            if start == 0:
                grads = [jnp.zeros((8, 128), F32) for _ in range(group)]
            else:
                grads = [grad_ref[(start + i, *at)] for i in range(group)]
            for i in range(group):
                for k in range(i):
                    gap = values[i] - values[k]
                    square = gap * gap + 0.25
                    inverse = lax.rsqrt(square)
                    pair = pair + inverse
                    slope = gap * inverse
                    grads[i] = grads[i] + slope
                    grads[k] = grads[k] - slope
            for m in range(start + group, members):
                other = value_ref[(m, *at)]
                if start == 0:
                    other_grad = jnp.zeros((8, 128), F32)
                else:
                    other_grad = grad_ref[(m, *at)]
                for i in range(group):
                    gap = other - values[i]
                    square = gap * gap + 0.25
                    inverse = lax.rsqrt(square)
                    pair = pair + inverse
                    slope = gap * inverse
                    other_grad = other_grad + slope
                    grads[i] = grads[i] - slope
                grad_ref[(m, *at)] = other_grad
            for i in range(group):
                miss = values[i] - truth
                square = miss * miss + 0.25
                inverse = lax.rsqrt(square)
                own = own + square * inverse
                moment = moment + values[i] * grads[i]
                answer = (miss * inverse) * (1.0 / members) + grads[i] * pair_scale
                grad_ref[(start + i, *at)] = answer * lat_weight
        pair = moment + 0.25 * pair
        return total + (own * (1.0 / members) + pair * pair_scale)

    tiles = (count // 8) * (channels // 128)
    total = lax.fori_loop(0, tiles, tile, jnp.zeros((8, 128), F32))
    loss_ref[...] = total * lat_weight
    slope_ref[...] = grad_ref[...].astype(BF16)


def call(kernel, out_shape, *operands, smem=(), away=(), away_out=(), loose=False, scratch=(), held=()):
    spaces = [pltpu.VMEM for _ in operands]
    for i in smem:
        spaces[i] = pltpu.SMEM
    for i in away:
        spaces[i] = pl.ANY
    operands = [
        pltpu.with_memory_space_constraint(x, pltpu.VMEM)
        if space == pltpu.VMEM and not loose
        else x
        for x, space in zip(operands, spaces)
    ]
    shapes = [
        shape if loose else (pltpu.VMEM if i in held else pltpu.HBM)(shape.shape, shape.dtype)
        for i, shape in enumerate(out_shape)
    ]
    out_spaces = [pltpu.VMEM for _ in shapes]
    for i in away_out:
        out_spaces[i] = pl.ANY
    return pl.pallas_call(
        kernel,
        out_shape=shapes,
        in_specs=[pl.BlockSpec(memory_space=space) for space in spaces],
        out_specs=[pl.BlockSpec(memory_space=space) for space in out_spaces],
        scratch_shapes=scratch,
        compiler_params=pltpu.CompilerParams(vmem_limit_bytes=None if loose else VMEM_LIMIT),
    )(*operands)


def reduce_weight_grad(mine, theirs, loss):
    lat_count, ens_count = lax.axis_size("lat"), lax.axis_size("ens")
    lon_index = lax.axis_index("lon")
    rows, lanes = mine.shape
    piece = rows // ens_count
    swap = [(0, 1), (1, 0)]
    arrived = lax.ppermute(theirs, "lon", swap)
    (summed,) = call(
        merge_kernel,
        (jax.ShapeDtypeStruct((ens_count, piece + 8, lanes), BF16),),
        mine,
        arrived,
        loss,
    )
    summed = lax.all_to_all(summed, "ens", 0, 0, tiled=True)

    total = jnp.sum(summed.astype(F32), 0)
    share = total[piece : piece + 1] + total[piece + 1 : piece + 2]
    blank = jnp.zeros((6, lanes), BF16)
    sent = jnp.concatenate([total[:piece].astype(BF16), *split(share), blank], 0)
    arrived = [
        lax.ppermute(sent, "lat", [(i, (i + step) % lat_count) for i in range(lat_count)])
        for step in range(1, lat_count)
    ]
    for block in arrived:
        total = total + block.astype(F32)
    spread_out = jnp.broadcast_to(
        total[None, :piece].astype(BF16), (ens_count, piece, lanes)
    )
    gathered = lax.all_to_all(spread_out, "ens", 0, 0, tiled=True)
    other = lax.ppermute(gathered, "lon", swap)
    shares = total[piece:]
    loss = jnp.sum((shares + lax.ppermute(shares, "lon", swap))[:2])
    (whole,) = call(
        whole_kernel,
        (jax.ShapeDtypeStruct((rows, 2 * lanes), F32),),
        gathered,
        other,
        lon_index[None],
        smem=(2,),
    )
    return whole, loss


def step(inputs, weight, spread, target):
    row_count, width, channels = inputs.shape[1:]
    reach = HMAX
    members = lax.axis_size("ens")
    lat_total = row_count * lax.axis_size("lat")
    lon_total = width * lax.axis_size("lon")
    lat_index, lon_index, ens_index = (lax.axis_index(a) for a in ("lat", "lon", "ens"))
    field = inputs[0]
    wave_cols, basis, all_basis = circle_waves(lon_index, width, lon_total)
    rows_around = lat_index * row_count - 1 + jnp.arange(row_count + 2)
    polar = (rows_around < PCAP) | (rows_around >= lat_total - PCAP)
    polar_scale = polar.astype(F32)

    spread_scale = spread.astype(F32)
    sums, parcel = call(
        parcel_kernel,
        (
            jax.ShapeDtypeStruct((row_count, 3, channels), F32),
            jax.ShapeDtypeStruct((row_count, 3 * reach, channels), BF16),
        ),
        field,
        all_basis,
        lon_index[None],
        smem=(2,),
        held=(0, 1),
    )
    other = lax.ppermute(parcel, "lon", [(0, 1), (1, 0)])
    (own,) = call(
        extend_kernel,
        (jax.ShapeDtypeStruct((row_count, width + 3 * reach, channels), BF16),),
        field,
        sums,
        other,
        spread_scale,
        smem=(3,),
        held=(0,),
    )
    low, high = lat_neighbours(own)
    own_band = band_blocks(spread, ~polar[1:3], reach)
    own_polar = polar_scale[1:3]
    cells = -(-(row_count * width // members) // 16) * 16
    (begun,) = call(
        own_rows_kernel,
        (jax.ShapeDtypeStruct((row_count, width, channels), F32),),
        own,
        weight,
        own_band,
        wave_cols,
        own_polar,
        smem=(4,),
        held=(0,),
    )
    response, sent = call(
        outer_rows_kernel,
        (
            jax.ShapeDtypeStruct((row_count, width, channels), BF16),
            jax.ShapeDtypeStruct((members * cells, channels), BF16),
        ),
        low,
        high,
        begun,
        weight,
        own_band,
        wave_cols,
        own_polar,
        smem=(6,),
    )
    everyone = lax.all_to_all(
        sent.reshape(members, cells, channels), "ens", 0, 0, tiled=True
    )
    held = row_count * width // cells
    first_cell = jnp.minimum(ens_index, held - 1) * cells
    truth = lax.dynamic_slice_in_dim(target.reshape(-1, channels), first_cell, cells, 0)
    cell_row = lat_index * row_count + first_cell // width
    row_weight = jnp.sin(math.pi * (cell_row.astype(F32) + 0.5) / lat_total)
    row_weight = jnp.where(ens_index < held, row_weight, 0.0)
    slopes, loss_tile = call(
        crps_kernel,
        (
            jax.ShapeDtypeStruct((members, cells, channels), BF16),
            jax.ShapeDtypeStruct((8, 128), F32),
        ),
        everyone,
        truth,
        row_weight[None],
        smem=(2,),
        held=(0, 1),
        scratch=[
            pltpu.VMEM((members, cells, channels), F32),
            pltpu.VMEM((members, cells, channels), F32),
        ],
    )
    slopes = lax.all_to_all(slopes, "ens", 0, 0, tiled=True)
    slopes = slopes.reshape(-1, channels)
    loss_share = jnp.sum(loss_tile, 0, keepdims=True) / (lat_total * lon_total * channels)

    slope_rows = slopes[: row_count * width].reshape(row_count, width, channels)
    slope_sums, slope_other = circle_parcel(slope_rows, basis, reach)
    scale = math.sqrt(weight.shape[0] * channels) / (lat_total * lon_total)
    half = jax.ShapeDtypeStruct((weight.shape[0] * channels, channels // 2), BF16)
    mine, theirs, slope_own = call(
        functools.partial(weight_grad_kernel, scale=scale),
        (half, half, jax.ShapeDtypeStruct((row_count, width + 3 * reach, channels), BF16)),
        slopes,
        slope_sums,
        slope_other,
        low,
        own,
        high,
        own_band,
        wave_cols,
        own_polar,
        lon_index[None],
        spread_scale,
        smem=(8, 9, 10),
        away=(0, 3, 4, 5),
        away_out=(0, 1),
        loose=True,
        scratch=[
            pltpu.VMEM((row_count, width, 3 * channels), BF16),
            pltpu.VMEM((row_count + 2, width, channels), BF16),
            pltpu.VMEM((2, *half.shape), BF16),
            pltpu.SemaphoreType.DMA((8,)),
        ],
    )
    slope_low, slope_high = lat_neighbours(slope_own)
    grad_weight, loss = reduce_weight_grad(mine, theirs, loss_share)
    around = jnp.stack([low[0, -1, 0], high[0, -1, 0]]).astype(spread.dtype)
    all_spread = jnp.concatenate([around[:1], spread, around[1:]])
    (grad_input,) = call(
        input_grad_kernel,
        (jax.ShapeDtypeStruct((row_count, width, channels), BF16),),
        slope_low,
        slope_own,
        slope_high,
        weight,
        band_blocks(all_spread, ~polar, reach),
        wave_cols,
        polar_scale,
        smem=(6,),
        loose=True,
        scratch=[pltpu.VMEM((row_count, width, channels), F32)],
    )
    return (response[None], grad_input[None], grad_weight.reshape(weight.shape), loss)


def solution(mesh):
    in_specs = (P("ens", "lat", "lon", None), P(), P("lat"), P("lat", "lon", None))
    out_specs = (P("ens", "lat", "lon", None), P("ens", "lat", "lon", None), P(), P())
    return jax.shard_map(step, mesh=mesh, in_specs=in_specs, out_specs=out_specs, check_vma=False)
```
